32 devices in a mesh: depth: 4 (over y, x), xline: 8 (over z, core).
Axes of the slice: x: 2, y: 2, z: 4, core: 2. Of those that a mesh axis runs over, the one named last changes fastest.
Arguments:
- receiver_data: bfloat16 [4, 2, 1024, 1024], P(None, None, None, 'xline'), may hold values from -6 to 6
- source_amp: bfloat16 [4, 2, 256], replicated, may hold values from -6 to 6
- source_x: int32 [256], replicated, may hold values from 0 to 1023
- source_y: int32 [256], replicated, may hold values from 0 to 1023
- omegas: float32 [4], replicated, may hold values from 0.5 to 3
- slowness: float32 [4, 1024, 1024], P('depth', None, 'xline'), may hold values from 0.2 to 2
- inverses: bfloat16 [4, 4, 2, 256, 256], replicated, may hold values from -0.1875 to 0.1875
- zones_x: int32 [4, 4], P('depth'), may hold values from 0 to 3
- zones_y: int32 [4, 4], P('depth'), may hold values from 0 to 3
Outputs:
- gradient: float32 [4, 1024, 1024], P('depth', None, 'xline')
The draws below stay inside these ranges and needn't reach their ends.
All inputs are finite; a program needn't handle non-finite values.
Results may differ from the reference program's by a relative error of at most 0.015.
Values may be sent and summed in bfloat16 or wider, within the bound.
A program may use at most 64 MiB of HBM per device.

```python
import math
import jax
import jax.numpy as jnp

NX = 1024
B = 256
NF = 4
ZONES = 4
NSRC = 256
NY = 1024
NZ = 4
NXB = 4
NYB = 4


def set_ends(drawn, key, low, high):
    spot = [jax.random.randint(jax.random.fold_in(key, axis), (), 0, length) for axis, length in enumerate(drawn.shape)]
    longest = drawn.shape.index(max(drawn.shape))
    neighbour = spot[:longest] + [(spot[longest] + 1) % drawn.shape[longest]] + spot[longest + 1:]
    return drawn.at[tuple(spot)].set(low).at[tuple(neighbour)].set(high)


def block_scale(stream_key, extent, split, low, top_value):
    loudness, own = 1.0, jax.random.fold_in(stream_key, 6)
    for dim, blocks in split:
        heights = jnp.exp(jax.random.uniform(jax.random.fold_in(own, dim), (blocks,), jnp.float32, low / len(split), top_value / len(split)))
        loudness = loudness * jnp.repeat(heights, extent[dim] // blocks).reshape([-1 if axis == dim else 1 for axis in range(len(extent))])
    return loudness


def bell_draw(key, dims, scale, reach, cuts=(), dtype=jnp.bfloat16):
    array = jax.random.normal(key, dims, jnp.float32) * scale
    if len(cuts) > 0:
        array = block_scale(key, dims, cuts, -0.22, 0.18) * array
    return jnp.clip(array, min=-reach, max=reach).astype(dtype)


def setup_inputs(seed: int = 0) -> dict:
    splits = jax.random.split(jax.random.key(seed), 10)
    receiver_data = bell_draw(splits[0], (NF, 2, NX, NY), 1.0, 6.0, ((3, 8),))
    source_amp = bell_draw(splits[1], (NF, 2, NSRC), 1.0, 6.0)
    source_x = set_ends(jax.random.randint(splits[2], (NSRC,), 0, NX), jax.random.fold_in(splits[2], 1), 0, NX - 1).astype(jnp.int32)
    source_y = set_ends(jax.random.randint(splits[3], (NSRC,), 0, NY), jax.random.fold_in(splits[3], 1), 0, NY - 1).astype(jnp.int32)
    omegas = jnp.clip(jnp.exp(jax.random.uniform(splits[4], (NF,), jnp.float32, math.log(0.5), math.log(3.0))), 0.5, 3.0)
    slowness = jnp.clip(0.2 + 1.8 * jax.random.uniform(splits[5], (NZ, NX, NY), jnp.float32) ** block_scale(splits[5], (NZ, NX, NY), ((0, 4), (2, 8)), -0.2, 0.2), 0.2, 2.0)
    inverses = bell_draw(splits[6], (NF, ZONES, 2, B, B), (4 * B) ** -0.5, 0.1875)
    zones_x = set_ends(jax.random.randint(splits[7], (NZ, NXB), 0, ZONES), jax.random.fold_in(splits[7], 1), 0, ZONES - 1).astype(jnp.int32)
    zones_y = set_ends(jax.random.randint(splits[8], (NZ, NYB), 0, ZONES), jax.random.fold_in(splits[8], 1), 0, ZONES - 1).astype(jnp.int32)
    return {"receiver_data": receiver_data, "source_amp": source_amp, "source_x": source_x, "source_y": source_y, "omegas": omegas, "slowness": slowness, "inverses": inverses, "zones_x": zones_x, "zones_y": zones_y}


def rotate(field, angle, sign):
    field_real = field[0].astype(jnp.float32)
    field_imag = field[1].astype(jnp.float32)
    cosine = jnp.cos(angle)
    sine = jnp.sin(angle) * sign
    return jnp.stack([field_real * cosine - field_imag * sine, field_real * sine + field_imag * cosine]).astype(jnp.bfloat16)


def solve_inline(field, blocks, sign):
    parts = field.astype(jnp.float32).reshape(2, NX // B, B, field.shape[2])
    k_real = blocks[:, 0].astype(jnp.float32)
    k_imag = sign * blocks[:, 1].astype(jnp.float32)
    def blockwise(matrix, vector):
        return jnp.einsum("bij,bjy->biy", matrix, vector)
    out_real = parts[0] + blockwise(k_real, parts[0]) - blockwise(k_imag, parts[1])
    out_imag = parts[1] + blockwise(k_real, parts[1]) + blockwise(k_imag, parts[0])
    return jnp.stack([out_real, out_imag]).reshape(field.shape).astype(jnp.bfloat16)


def solve_crossline(field, blocks, sign):
    parts = field.astype(jnp.float32).reshape(2, field.shape[1], NY // B, B)
    k_real = blocks[:, 0].astype(jnp.float32)
    k_imag = sign * blocks[:, 1].astype(jnp.float32)
    def blockwise(matrix, vector):
        return jnp.einsum("bij,xbj->xbi", matrix, vector)
    out_real = parts[0] + blockwise(k_real, parts[0]) - blockwise(k_imag, parts[1])
    out_imag = parts[1] + blockwise(k_real, parts[1]) + blockwise(k_imag, parts[0])
    return jnp.stack([out_real, out_imag]).reshape(field.shape).astype(jnp.bfloat16)


def continue_level(field, angle, table, zone_row_x, zone_row_y, sign):
    rotated = rotate(field, angle, sign)
    inline = solve_inline(rotated, jnp.take(table, zone_row_x, axis=0), sign)
    return solve_crossline(inline, jnp.take(table, zone_row_y, axis=0), sign)


def reference(receiver_data, source_amp, source_x, source_y, omegas, slowness, inverses, zones_x, zones_y):
    source_all = jnp.zeros((NF, 2, NX, NY), jnp.float32).at[:, :, source_x, source_y].add(source_amp.astype(jnp.float32))
    source_all = source_all.astype(jnp.bfloat16)
    gradient = jnp.zeros((NZ, NX, NY), jnp.float32)
    for freq in range(NF):
        source_field = source_all[freq]
        receiver_field = receiver_data[freq]
        weight = omegas[freq] * omegas[freq]
        for level in range(NZ):
            angle = omegas[freq] * slowness[level]
            source_field = continue_level(source_field, angle, inverses[freq], zones_x[level], zones_y[level], 1.0)
            receiver_field = continue_level(receiver_field, angle, inverses[freq], zones_x[level], zones_y[level], -1.0)
            correlation = source_field[0].astype(jnp.float32) * receiver_field[0].astype(jnp.float32) + source_field[1].astype(jnp.float32) * receiver_field[1].astype(jnp.float32)
            gradient = gradient.at[level].add(weight * correlation)
    return gradient
```

```python
import functools
import math

import jax
import jax.numpy as jnp
import numpy as np
from jax import lax
from jax.experimental import pallas as pl
from jax.experimental.pallas import tpu as pltpu
from jax.sharding import PartitionSpec as P

MESH = pl.DeviceIdType.MESH
F32 = jnp.float32
BF16 = jnp.bfloat16

SLOW_LOW, SLOW_HIGH = 0.2, 2.0
OMEGA_LOW, OMEGA_HIGH = 0.5, 3.0
SLOW_MID = 0.5 * (SLOW_LOW + SLOW_HIGH)
CODE_STEP = (SLOW_HIGH - SLOW_LOW) / 65532.0
HALF_SPAN = 0.5 * max(OMEGA_HIGH * SLOW_HIGH - math.pi, math.pi - OMEGA_LOW * SLOW_LOW) + 0.01


def fitted(function, count):
    nodes = np.cos(np.pi * (np.arange(64) + 0.5) / 64)
    square = 0.5 * HALF_SPAN**2 * (nodes + 1.0)
    fit = np.polynomial.Chebyshev.fit(square, function(np.sqrt(square)), count - 1)
    return [float(term) for term in fit.convert(kind=np.polynomial.Polynomial).coef]


PARTS = 2
ROOT2 = math.sqrt(2.0)
SIN_TERMS = fitted(lambda t: ROOT2 * np.sin(t) / t, 5)
COS_TERMS = fitted(lambda t: -ROOT2 * np.cos(t), 5)


def series(square, terms):
    total = square * terms[-1] + terms[-2]
    for term in terms[-3::-1]:
        total = total * square + term
    return total


def sincos(half):
    square = half * half
    root_sine = series(square, SIN_TERMS) * half
    return root_sine * series(square, COS_TERMS), root_sine * root_sine - 1.0


def block_form(blocks):
    k_real, k_imag = blocks[0], blocks[1]
    top = jnp.concatenate([k_real, -k_imag], axis=1)
    bottom = jnp.concatenate([k_imag, k_real], axis=1)
    return jnp.concatenate([top, bottom], axis=0)


def kernel(
    sections, pair, rows, recv_in, amp_in, src_x_in, src_y_in, omegas_in, slow_in, table_in,
    zones_x_in, zones_y_in,
    out, slow, slow_raw, code, rec, wave, table, amp, src_x, src_y, omegas, zones_x, zones_y,
    zones, zone_buf, zone_rows, trig, rotated, inline, grad, got, total,
    load_sems, local_sems, zone_sems, zone_send, zone_recv, slow_send, slow_recv, fwd_send, fwd_recv,
    rec_send, rec_recv, swap_send, swap_recv, last_send, last_recv, grad_send, grad_recv, tail_send,
    tail_recv, ready,
):
    d = lax.axis_index("depth")
    line = lax.axis_index("xline")
    q = lax.rem(line, pair)
    block = line // pair
    mate_line = line + 1 - 2 * q
    width = recv_in.shape[3]
    order = pair * width
    slots = wave.shape[0]
    last = sections - 1
    parts = last_send.shape[0]
    mine = pl.ds(pl.multiple_of(q * width, width), width)
    theirs = pl.ds(pl.multiple_of((1 - q) * width, width), width)

    def rows_of(section):
        return pl.ds(pl.multiple_of(section * order, order), order)

    near = d + 1 - 2 * lax.rem(d, 2)
    next_to = d + 2 - 4 * (d // 2)
    far = last - d
    others = [far, near, next_to]
    FAR, NEAR, NEXT = range(3)

    barrier = pltpu.get_barrier_semaphore()
    for device in ((near, line), (next_to, line), (d, mate_line)):
        pl.semaphore_signal(barrier, inc=1, device_id=device, device_id_type=MESH)

    freqs = pl.ds(q * slots, slots)
    loads = [
        pltpu.make_async_copy(
            slow_in.at[0, rows_of(section), :], slow_raw.at[rows_of(section), :], load_sems.at[k]
        )
        for k, section in enumerate(others + [d])
    ]
    small = [
        pltpu.make_async_copy(source, target, local_sems.at[k])
        for k, (source, target) in enumerate((
            (zones_x_in, zones_x), (zones_y_in, zones_y), (omegas_in, omegas),
            (amp_in, amp), (src_x_in, src_x), (src_y_in, src_y),
        ))
    ]
    rec_load = pltpu.make_async_copy(
        recv_in.at[freqs, :, rows_of(d), :], rec.at[:, :, :, mine], local_sems.at[len(small)]
    )
    table_load = pltpu.make_async_copy(
        table_in.at[freqs], table, local_sems.at[len(small) + 1]
    )
    for copy in loads + small + [rec_load]:
        copy.start()

    def encode(section):
        part = rows_of(section)
        scaled = (slow_raw[part, :] - SLOW_MID) * (1.0 / CODE_STEP)
        return jnp.round(scaled).astype(jnp.int32).astype(jnp.int16)

    zones[...] = jnp.zeros_like(zones)
    small[0].wait()
    small[1].wait()
    zones[0:1, 0:zones_x.shape[1]] = zones_x[...]
    zones[1:2, 0:zones_y.shape[1]] = zones_y[...]
    zone_buf[d] = zones[...]
    for k, section in enumerate(others):
        loads[k].wait()
        code[rows_of(section), :] = encode(section)
    loads[len(others)].wait()
    slow[d, :, mine] = encode(d)
    table_load.start()

    zone_copies, slow_copies = [], []
    for k, other in enumerate(others):
        zone_copies.append(
            pltpu.make_async_remote_copy(
                src_ref=zones, dst_ref=zone_buf.at[d], send_sem=zone_send.at[k],
                recv_sem=zone_recv.at[d], device_id=(other, line), device_id_type=MESH,
            )
        )
        slow_copies.append(
            pltpu.make_async_remote_copy(
                src_ref=code.at[rows_of(other), :], dst_ref=slow.at[d, :, mine],
                send_sem=slow_send.at[k], recv_sem=slow_recv.at[d],
                device_id=(other, line), device_id_type=MESH,
            )
        )
    rec_copy = pltpu.make_async_remote_copy(
        src_ref=recv_in.at[pl.ds((1 - q) * slots, slots), :, rows_of(d), :],
        dst_ref=rec.at[:, :, :, mine], send_sem=rec_send, recv_sem=rec_recv,
        device_id=(d, mate_line), device_id_type=MESH,
    )

    def share(k):
        zone_copies[k].start()
        slow_copies[k].start()

    def arrived(level):
        zone = pltpu.make_async_remote_copy(
            src_ref=zones, dst_ref=zone_buf.at[level], send_sem=zone_send.at[0],
            recv_sem=zone_recv.at[level], device_id=(d, mate_line), device_id_type=MESH,
        )
        rest = pltpu.make_async_remote_copy(
            src_ref=slow.at[level, :, mine], dst_ref=slow.at[level, :, mine],
            send_sem=slow_send.at[0], recv_sem=slow_recv.at[level],
            device_id=(d, mate_line), device_id_type=MESH,
        )
        return zone, rest

    def forward(level, half):
        return pltpu.make_async_remote_copy(
            src_ref=slow.at[level, :, half], dst_ref=slow.at[level, :, half],
            send_sem=fwd_send.at[level], recv_sem=fwd_recv.at[level],
            device_id=(d, mate_line), device_id_type=MESH,
        )

    def zone_copy(level):
        return pltpu.make_async_copy(
            zone_buf.at[level], zone_rows.at[level], zone_sems.at[level]
        )

    def receive(level):
        @pl.when(level != d)
        def _():
            for copy in arrived(level):
                copy.wait_recv()
        zone_copy(level).start()
        forward(level, mine).start()

    pl.semaphore_wait(barrier, pair + 1)
    pl.semaphore_signal(ready, inc=1, device_id=(near, line), device_id_type=MESH)

    @pl.when(d == 0)
    def _():
        share(NEAR)
        share(NEXT)

    @pl.when(d != 0)
    def _():
        pl.semaphore_wait(ready, 1)
        share(FAR)
        share(NEAR)
        share(NEXT)

    rec_copy.start()
    for copy in small[2:]:
        copy.wait()

    points = src_x.shape[1]
    cells = lax.broadcasted_iota(jnp.int32, (order, points), 0)
    hit_x = cells + d * order == src_x[...]
    hit_y = jnp.where(cells + block * order == src_y[...], 1.0, 0.0).astype(BF16)
    for slot in range(slots):
        for part in range(2):
            amps = amp[q * slots + slot, pl.ds(part, 1), :].astype(F32)
            spread = jnp.where(hit_x, amps, 0.0).astype(BF16)
            field = lax.dot_general(
                spread, hit_y, (((1,), (1,)), ((), ())), preferred_element_type=F32
            )
            wave[slot, 0, part] = field.astype(BF16)

    @pl.when(d == 0)
    def _():
        pl.semaphore_wait(ready, 1)
        share(FAR)

    def turn(level, slot, lanes):
        omega = omegas[q * slots + slot]
        slope = omega * (0.5 * CODE_STEP)
        shift = omega * (0.5 * SLOW_MID) - 0.5 * math.pi
        for start in range(0, order, rows):
            part = slice(start, start + rows)
            value = slow[level, part, lanes].astype(jnp.int32).astype(F32)
            sine, cosine = sincos(value * slope + shift)
            trig[slot, 0, part, lanes] = sine
            trig[slot, 1, part, lanes] = cosine

    def rotate(slot):
        for start in range(0, order, rows):
            part = slice(start, start + rows)
            sine, cosine = trig[slot, 0, part, :], trig[slot, 1, part, :]
            for field in range(2):
                real = wave[slot, field, 0, part, :].astype(F32)
                imag = wave[slot, field, 1, part, :].astype(F32)
                lanes = slice(field * order, (field + 1) * order)
                rotated[slot, part, lanes] = (real * cosine - imag * sine).astype(BF16)
                rotated[slot, order + start:order + start + rows, lanes] = (
                    real * sine + imag * cosine
                ).astype(BF16)

    def solve_inline(level, slot):
        m_x = block_form(table[slot, zone_rows[level, 0, d]])
        for field in range(2):
            lanes = slice(field * order, (field + 1) * order)
            value = rotated[slot, :, lanes]
            solved = value.astype(F32) + jnp.dot(m_x, value, preferred_element_type=F32)
            solved = solved.astype(BF16)
            inline[slot, lanes, 0:order] = solved[:order]
            inline[slot, lanes, order:] = solved[order:]

    def solve_crossline(level, slot, part):
        omega = omegas[q * slots + slot]
        m_y = block_form(table[slot, zone_rows[level, 1, block]])
        count = part.stop - part.start
        value = jnp.concatenate(
            [inline[slot, part, :], inline[slot, order + part.start:order + part.stop, :]], axis=0
        )
        product = []
        for half in range(2):
            lanes = slice(half * order, (half + 1) * order)
            solved = value[:, lanes].astype(F32) + lax.dot_general(
                value, m_y[lanes], (((1,), (1,)), ((), ())), preferred_element_type=F32
            )
            product.append(solved[:count] * solved[count:])
            if level < last:
                wave[slot, 0, half, part] = solved[:count].astype(BF16)
                wave[slot, 1, half, part] = solved[count:].astype(BF16)
        image = (omega * omega) * (product[0] - product[1])
        if slot > 0:
            image = total[part, :] + image
        if slot + 1 < slots:
            total[part, :] = image
        else:
            grad[level, part, :] = image.astype(BF16)

    def swap(level):
        return pltpu.make_async_remote_copy(
            src_ref=grad.at[level, :, theirs], dst_ref=got.at[level],
            send_sem=swap_send.at[level], recv_sem=swap_recv.at[level],
            device_id=(d, mate_line), device_id_type=MESH,
        )

    def swap_part(k):
        part = pl.ds(k * (order // parts), order // parts)
        return pltpu.make_async_remote_copy(
            src_ref=grad.at[last, part, theirs], dst_ref=got.at[last, part],
            send_sem=last_send.at[k], recv_sem=last_recv.at[k],
            device_id=(d, mate_line), device_id_type=MESH,
        )

    def deliver_copy(level):
        return pltpu.make_async_remote_copy(
            src_ref=got.at[level], dst_ref=out.at[rows_of(d), :],
            send_sem=grad_send.at[level], recv_sem=grad_recv.at[d],
            device_id=(level, line), device_id_type=MESH,
        )

    def section_part(section, k):
        count = order // parts
        return pl.ds(pl.multiple_of(section * order + k * count, count), count)

    def deliver_part(k, section):
        part = pl.ds(k * (order // parts), order // parts)
        return pltpu.make_async_remote_copy(
            src_ref=got.at[last, part], dst_ref=out.at[section_part(section, k), :],
            send_sem=tail_send.at[k], recv_sem=tail_recv.at[section, k],
            device_id=(last, line), device_id_type=MESH,
        )

    def deliver(level):
        swap(level).wait_recv()
        both = grad[level, :, mine].astype(F32) + got[level].astype(F32)

        @pl.when(level == d)
        def _():
            out[rows_of(d), :] = both.astype(BF16)

        @pl.when(level != d)
        def _():
            got[level] = both.astype(BF16)
            deliver_copy(level).start()

    def deliver_last(k):
        part = pl.ds(k * (order // parts), order // parts)
        swap_part(k).wait_recv()
        both = grad[last, part, mine].astype(F32) + got[last, part].astype(F32)

        @pl.when(d == last)
        def _():
            out[section_part(d, k), :] = both.astype(BF16)

        @pl.when(d != last)
        def _():
            got[last, part] = both.astype(BF16)
            deliver_part(k, d).start()

    whole = slice(0, order)
    rec_load.wait()
    rec_copy.wait_recv()
    for slot in range(slots):
        wave[slot, 1, 0] = rec[slot, 0]
        wave[slot, 1, 1] = -rec[slot, 1]
    table_load.wait()

    receive(0)
    for slot in range(slots):
        turn(0, slot, mine)
    if sections > 1:
        receive(1)
    zone_copy(0).wait()
    forward(0, theirs).wait_recv()
    for slot in range(slots):
        turn(0, slot, theirs)
    for slot in range(slots):
        rotate(slot)
        solve_inline(0, slot)

    for level in range(1, sections):
        if level + 1 < sections:
            receive(level + 1)
        if level > 1:
            swap(level - 2).start()
        if level > 2:
            deliver(level - 3)
        zone_copy(level).wait()
        forward(level, theirs).wait_recv()
        for slot in range(slots):
            solve_crossline(level - 1, slot, whole)
            turn(level, slot, whole)
        for slot in range(slots):
            rotate(slot)
            solve_inline(level, slot)
    swap(last - 1).start()
    for k in range(parts):
        part = slice(k * (order // parts), (k + 1) * (order // parts))
        for slot in range(slots):
            solve_crossline(last, slot, part)
        swap_part(k).start()
        if k == 0:
            for level in range(max(last - 2, 0), last):
                deliver(level)
    for k in range(parts):
        deliver_last(k)

    for copy in zone_copies + slow_copies:
        copy.wait_send()
    rec_copy.wait_send()
    for level in range(sections):
        forward(level, mine).wait_send()
    for level in range(last):
        swap(level).wait_send()

        @pl.when(level != d)
        def _():
            deliver_copy(level).wait_send()
    for k in range(parts):
        swap_part(k).wait_send()

    @pl.when(d != last)
    def _():
        for k in range(parts):
            deliver_part(k, d).wait_send()
        for other in others:
            pltpu.make_async_remote_copy(
                src_ref=got.at[0], dst_ref=out.at[rows_of(other), :],
                send_sem=grad_send.at[0], recv_sem=grad_recv.at[other],
                device_id=(d, mate_line), device_id_type=MESH,
            ).wait_recv()

    @pl.when(d == last)
    def _():
        for other in others:
            for k in range(parts):
                deliver_part(k, other).wait_recv()


def per_device(
    receiver_data, source_amp, source_x, source_y, omegas, slowness, inverses, zones_x, zones_y
):
    sections = lax.axis_size("depth")
    freqs, _, width_x, width_y = receiver_data.shape
    order = inverses.shape[-1]
    pair = order // width_y
    points = source_x.shape[0]
    zone_count = inverses.shape[1]
    slots = freqs // pair
    assert pair == 2 and sections == 4 and width_x == order * sections and slowness.shape[0] == 1
    vmem = pl.BlockSpec(memory_space=pltpu.VMEM)
    anywhere = pl.BlockSpec(memory_space=pl.ANY)
    dma = pltpu.SemaphoreType.DMA
    out = pl.pallas_call(
        functools.partial(kernel, sections, pair, 32),
        out_shape=pltpu.VMEM((width_x, width_y), BF16),
        in_specs=[anywhere] * 9,
        out_specs=vmem,
        scratch_shapes=[
            pltpu.VMEM((sections, order, order), jnp.int16),
            pltpu.VMEM((width_x, width_y), F32),
            pltpu.VMEM((width_x, width_y), jnp.int16),
            pltpu.VMEM((slots, 2, order, order), BF16),
            pltpu.VMEM((slots, 2, 2, order, order), BF16),
            pltpu.VMEM((slots, zone_count, 2, order, order), BF16),
            pltpu.VMEM(source_amp.shape, BF16),
            pltpu.VMEM((1, points), jnp.int32),
            pltpu.VMEM((1, points), jnp.int32),
            pltpu.SMEM(omegas.shape, F32),
            pltpu.VMEM(zones_x.shape, jnp.int32),
            pltpu.VMEM(zones_y.shape, jnp.int32),
            pltpu.VMEM((8, 128), jnp.int32),
            pltpu.VMEM((sections, 8, 128), jnp.int32),
            pltpu.SMEM((sections, 8, 128), jnp.int32),
            pltpu.VMEM((slots, 2, order, order), F32),
            pltpu.VMEM((slots, 2 * order, 2 * order), BF16),
            pltpu.VMEM((slots, 2 * order, 2 * order), BF16),
            pltpu.VMEM((sections, order, order), BF16),
            pltpu.VMEM((sections, order, width_y), BF16),
            pltpu.VMEM((order, order), F32),
            dma((sections,)), dma((8,)), dma((sections,)),
            dma((sections,)), dma((sections,)),
            dma((sections,)), dma((sections,)),
            dma((sections,)), dma((sections,)),
            dma, dma,
            dma((sections,)), dma((sections,)),
            dma((PARTS,)), dma((PARTS,)),
            dma((sections,)), dma((sections,)),
            dma((PARTS,)), dma((sections, PARTS)),
            pltpu.SemaphoreType.REGULAR,
        ],
        compiler_params=pltpu.CompilerParams(collective_id=0, has_side_effects=True),
    )(
        receiver_data, source_amp, source_x.reshape(1, points), source_y.reshape(1, points),
        omegas, slowness, inverses, zones_x, zones_y,
    )
    return out.astype(F32)[None]


def solution(mesh):
    in_specs = (
        P(None, None, None, "xline"),
        P(),
        P(),
        P(),
        P(),
        P("depth", None, "xline"),
        P(),
        P("depth", None),
        P("depth", None),
    )
    out_specs = P("depth", None, "xline")
    return jax.shard_map(
        per_device, mesh=mesh, in_specs=in_specs, out_specs=out_specs, check_vma=False
    )
```

```python
import functools
import math

import jax
import jax.numpy as jnp
import numpy as np
from jax import lax
from jax.experimental import pallas as pl
from jax.experimental.pallas import tpu as pltpu
from jax.sharding import PartitionSpec as P

MESH = pl.DeviceIdType.MESH
F32 = jnp.float32
BF16 = jnp.bfloat16

SLOW_LOW, SLOW_HIGH = 0.2, 2.0
OMEGA_LOW, OMEGA_HIGH = 0.5, 3.0
SLOW_MID = 0.5 * (SLOW_LOW + SLOW_HIGH)
CODE_STEP = (SLOW_HIGH - SLOW_LOW) / 65532.0
HALF_SPAN = 0.5 * max(OMEGA_HIGH * SLOW_HIGH - math.pi, math.pi - OMEGA_LOW * SLOW_LOW) + 0.01


def fitted(function, count):
    nodes = np.cos(np.pi * (np.arange(64) + 0.5) / 64)
    square = 0.5 * HALF_SPAN**2 * (nodes + 1.0)
    fit = np.polynomial.Chebyshev.fit(square, function(np.sqrt(square)), count - 1)
    return [float(term) for term in fit.convert(kind=np.polynomial.Polynomial).coef]


PARTS = 2
ROOT2 = math.sqrt(2.0)
SIN_TERMS = fitted(lambda t: ROOT2 * np.sin(t) / t, 4)
COS_TERMS = fitted(lambda t: -ROOT2 * np.cos(t), 5)


def series(square, terms):
    total = square * terms[-1] + terms[-2]
    for term in terms[-3::-1]:
        total = total * square + term
    return total


def sincos(half):
    square = half * half
    root_sine = series(square, SIN_TERMS) * half
    return root_sine * series(square, COS_TERMS), root_sine * root_sine - 1.0


def kernel(
    sections, pair, rows, recv_in, amp_in, src_x_in, src_y_in, omegas_in, slow_in, table_in,
    zones_x_in, zones_y_in,
    out, slow, slow_raw, code, rec, wave, table, forms, amp, src_x, src_y, omegas, zones_x, zones_y,
    zones, zone_buf, zone_rows, trig, rotated, inline, grad, got, total,
    load_sems, local_sems, zone_sems, zone_send, zone_recv, slow_send, slow_recv, fwd_send, fwd_recv,
    rec_send, rec_recv, swap_send, swap_recv, last_send, last_recv, grad_send, grad_recv, tail_send,
    tail_recv, ready,
):
    d = lax.axis_index("depth")
    line = lax.axis_index("xline")
    q = lax.rem(line, pair)
    block = line // pair
    mate_line = line + 1 - 2 * q
    width = recv_in.shape[3]
    order = pair * width
    slots = wave.shape[0]
    last = sections - 1
    parts = last_send.shape[0]
    mine = pl.ds(pl.multiple_of(q * width, width), width)
    theirs = pl.ds(pl.multiple_of((1 - q) * width, width), width)

    def rows_of(section):
        return pl.ds(pl.multiple_of(section * order, order), order)

    near = d + 1 - 2 * lax.rem(d, 2)
    next_to = d + 2 - 4 * (d // 2)
    far = last - d
    others = [far, near, next_to]
    FAR, NEAR, NEXT = range(3)

    barrier = pltpu.get_barrier_semaphore()
    for device in ((near, line), (next_to, line), (d, mate_line)):
        pl.semaphore_signal(barrier, inc=1, device_id=device, device_id_type=MESH)

    freqs = pl.ds(q * slots, slots)
    loads = [
        pltpu.make_async_copy(
            slow_in.at[0, rows_of(section), :], slow_raw.at[rows_of(section), :], load_sems.at[k]
        )
        for k, section in enumerate(others + [d])
    ]
    small = [
        pltpu.make_async_copy(source, target, local_sems.at[k])
        for k, (source, target) in enumerate((
            (zones_x_in, zones_x), (zones_y_in, zones_y), (omegas_in, omegas),
            (amp_in, amp), (src_x_in, src_x), (src_y_in, src_y),
        ))
    ]
    rec_load = pltpu.make_async_copy(
        recv_in.at[freqs, :, rows_of(d), :], rec.at[:, :, :, mine], local_sems.at[len(small)]
    )
    table_load = pltpu.make_async_copy(
        table_in.at[freqs], table, local_sems.at[len(small) + 1]
    )
    for copy in loads + small + [rec_load]:
        copy.start()

    def encode(section):
        part = rows_of(section)
        scaled = (slow_raw[part, :] - SLOW_MID) * (1.0 / CODE_STEP)
        return jnp.round(scaled).astype(jnp.int32).astype(jnp.int16)

    zones[...] = jnp.zeros_like(zones)
    small[0].wait()
    small[1].wait()
    zones[0:1, 0:zones_x.shape[1]] = zones_x[...]
    zones[1:2, 0:zones_y.shape[1]] = zones_y[...]
    zone_buf[d] = zones[...]
    for k, section in enumerate(others):
        loads[k].wait()
        code[rows_of(section), :] = encode(section)
    loads[len(others)].wait()
    slow[d, :, mine] = encode(d)
    table_load.start()

    zone_copies, slow_copies = [], []
    for k, other in enumerate(others):
        zone_copies.append(
            pltpu.make_async_remote_copy(
                src_ref=zones, dst_ref=zone_buf.at[d], send_sem=zone_send.at[k],
                recv_sem=zone_recv.at[d], device_id=(other, line), device_id_type=MESH,
            )
        )
        slow_copies.append(
            pltpu.make_async_remote_copy(
                src_ref=code.at[rows_of(other), :], dst_ref=slow.at[d, :, mine],
                send_sem=slow_send.at[k], recv_sem=slow_recv.at[d],
                device_id=(other, line), device_id_type=MESH,
            )
        )
    rec_copy = pltpu.make_async_remote_copy(
        src_ref=recv_in.at[pl.ds((1 - q) * slots, slots), :, rows_of(d), :],
        dst_ref=rec.at[:, :, :, mine], send_sem=rec_send, recv_sem=rec_recv,
        device_id=(d, mate_line), device_id_type=MESH,
    )

    def share(k):
        zone_copies[k].start()
        slow_copies[k].start()

    def arrived(level):
        zone = pltpu.make_async_remote_copy(
            src_ref=zones, dst_ref=zone_buf.at[level], send_sem=zone_send.at[0],
            recv_sem=zone_recv.at[level], device_id=(d, mate_line), device_id_type=MESH,
        )
        rest = pltpu.make_async_remote_copy(
            src_ref=slow.at[level, :, mine], dst_ref=slow.at[level, :, mine],
            send_sem=slow_send.at[0], recv_sem=slow_recv.at[level],
            device_id=(d, mate_line), device_id_type=MESH,
        )
        return zone, rest

    def forward(level, half):
        return pltpu.make_async_remote_copy(
            src_ref=slow.at[level, :, half], dst_ref=slow.at[level, :, half],
            send_sem=fwd_send.at[level], recv_sem=fwd_recv.at[level],
            device_id=(d, mate_line), device_id_type=MESH,
        )

    def zone_copy(level):
        return pltpu.make_async_copy(
            zone_buf.at[level], zone_rows.at[level], zone_sems.at[level]
        )

    def receive(level):
        @pl.when(level != d)
        def _():
            for copy in arrived(level):
                copy.wait_recv()
        zone_copy(level).start()
        forward(level, mine).start()

    pl.semaphore_wait(barrier, pair + 1)
    pl.semaphore_signal(ready, inc=1, device_id=(near, line), device_id_type=MESH)

    share(NEAR)
    share(NEXT)
    rec_copy.start()
    for copy in small[2:]:
        copy.wait()

    points = src_x.shape[1]
    cells = lax.broadcasted_iota(jnp.int32, (order, points), 0)
    hit_x = cells + d * order == src_x[...]
    hit_y = jnp.where(cells + block * order == src_y[...], 1.0, 0.0).astype(BF16)
    for slot in range(slots):
        for part in range(2):
            amps = amp[q * slots + slot, pl.ds(part, 1), :].astype(F32)
            spread = jnp.where(hit_x, amps, 0.0).astype(BF16)
            field = lax.dot_general(
                spread, hit_y, (((1,), (1,)), ((), ())), preferred_element_type=F32
            )
            wave[slot, 0, part] = field.astype(BF16)

    pl.semaphore_wait(ready, 1)
    share(FAR)

    table_load.wait()
    for slot in range(slots):
        for zone in range(table.shape[1]):
            k_real, k_imag = table[slot, zone, 0], table[slot, zone, 1]
            forms[slot, zone, :order, :order] = k_real
            forms[slot, zone, :order, order:] = -k_imag
            forms[slot, zone, order:, :order] = k_imag
            forms[slot, zone, order:, order:] = k_real

    def turn(level, lanes):
        for start in range(0, order, rows):
            part = slice(start, start + rows)
            value = slow[level, part, lanes].astype(jnp.int32).astype(F32)
            for slot in range(slots):
                omega = omegas[q * slots + slot]
                slope = omega * (0.5 * CODE_STEP)
                shift = omega * (0.5 * SLOW_MID) - 0.5 * math.pi
                sine, cosine = sincos(value * slope + shift)
                trig[slot, 0, part, lanes] = sine.astype(BF16)
                trig[slot, 1, part, lanes] = cosine.astype(BF16)

    def rotate(slot):
        for start in range(0, order, rows):
            part = slice(start, start + rows)
            sine, cosine = trig[slot, 0, part, :], trig[slot, 1, part, :]
            for field in range(2):
                real, imag = wave[slot, field, 0, part, :], wave[slot, field, 1, part, :]
                lanes = slice(field * order, (field + 1) * order)
                rotated[slot, part, lanes] = real * cosine - imag * sine
                rotated[slot, order + start:order + start + rows, lanes] = (
                    real * sine + imag * cosine
                )

    def solve_inline(level, slot):
        m_x = forms[slot, zone_rows[level, 0, d]]
        for field in range(2):
            lanes = slice(field * order, (field + 1) * order)
            value = rotated[slot, :, lanes]
            added = jnp.dot(m_x, value, preferred_element_type=F32).astype(BF16)
            solved = value + added
            inline[slot, lanes, 0:order] = solved[:order]
            inline[slot, lanes, order:] = solved[order:]

    def solve_crossline(level, slot, part):
        omega = omegas[q * slots + slot]
        m_y = forms[slot, zone_rows[level, 1, block]]
        count = part.stop - part.start
        value = jnp.concatenate(
            [inline[slot, part, :], inline[slot, order + part.start:order + part.stop, :]], axis=0
        )
        product = []
        for half in range(2):
            lanes = slice(half * order, (half + 1) * order)
            added = lax.dot_general(
                value, m_y[lanes], (((1,), (1,)), ((), ())), preferred_element_type=F32
            )
            solved = value[:, lanes] + added.astype(BF16)
            product.append(solved[:count].astype(F32) * solved[count:].astype(F32))
            if level < last:
                wave[slot, 0, half, part] = solved[:count]
                wave[slot, 1, half, part] = solved[count:]
        image = (omega * omega) * (product[0] - product[1])
        if slot > 0:
            image = total[part, :] + image
        if slot + 1 < slots:
            total[part, :] = image
        else:
            grad[level, part, :] = image.astype(BF16)

    def swap(level):
        return pltpu.make_async_remote_copy(
            src_ref=grad.at[level, :, theirs], dst_ref=got.at[level],
            send_sem=swap_send.at[level], recv_sem=swap_recv.at[level],
            device_id=(d, mate_line), device_id_type=MESH,
        )

    def swap_part(k):
        part = pl.ds(k * (order // parts), order // parts)
        return pltpu.make_async_remote_copy(
            src_ref=grad.at[last, part, theirs], dst_ref=got.at[last, part],
            send_sem=last_send.at[k], recv_sem=last_recv.at[k],
            device_id=(d, mate_line), device_id_type=MESH,
        )

    def deliver_copy(level):
        return pltpu.make_async_remote_copy(
            src_ref=got.at[level], dst_ref=out.at[rows_of(d), :],
            send_sem=grad_send.at[level], recv_sem=grad_recv.at[d],
            device_id=(level, line), device_id_type=MESH,
        )

    def section_part(section, k):
        count = order // parts
        return pl.ds(pl.multiple_of(section * order + k * count, count), count)

    def deliver_part(k, section):
        part = pl.ds(k * (order // parts), order // parts)
        return pltpu.make_async_remote_copy(
            src_ref=got.at[last, part], dst_ref=out.at[section_part(section, k), :],
            send_sem=tail_send.at[k], recv_sem=tail_recv.at[section, k],
            device_id=(last, line), device_id_type=MESH,
        )

    def deliver(level):
        swap(level).wait_recv()
        both = grad[level, :, mine].astype(F32) + got[level].astype(F32)

        @pl.when(level == d)
        def _():
            out[rows_of(d), :] = both.astype(BF16)

        @pl.when(level != d)
        def _():
            got[level] = both.astype(BF16)
            deliver_copy(level).start()

    def deliver_last(k):
        part = pl.ds(k * (order // parts), order // parts)
        swap_part(k).wait_recv()
        both = grad[last, part, mine].astype(F32) + got[last, part].astype(F32)

        @pl.when(d == last)
        def _():
            out[section_part(d, k), :] = both.astype(BF16)

        @pl.when(d != last)
        def _():
            got[last, part] = both.astype(BF16)
            deliver_part(k, d).start()

    whole = slice(0, order)
    rec_load.wait()
    rec_copy.wait_recv()
    for slot in range(slots):
        wave[slot, 1, 0] = rec[slot, 0]
        wave[slot, 1, 1] = -rec[slot, 1]
    receive(0)
    turn(0, mine)
    if sections > 1:
        receive(1)
    zone_copy(0).wait()
    forward(0, theirs).wait_recv()
    turn(0, theirs)
    for slot in range(slots):
        rotate(slot)
        solve_inline(0, slot)

    for level in range(1, sections):
        if level + 1 < sections:
            receive(level + 1)
        if level > 1:
            swap(level - 2).start()
        if level > 2:
            deliver(level - 3)
        zone_copy(level).wait()
        forward(level, theirs).wait_recv()
        for slot in range(slots):
            solve_crossline(level - 1, slot, whole)
        turn(level, whole)
        for slot in range(slots):
            rotate(slot)
            solve_inline(level, slot)
    swap(last - 1).start()
    for k in range(parts):
        part = slice(k * (order // parts), (k + 1) * (order // parts))
        for slot in range(slots):
            solve_crossline(last, slot, part)
        swap_part(k).start()
        if k == 0:
            for level in range(max(last - 2, 0), last):
                deliver(level)
    for k in range(parts):
        deliver_last(k)

    for copy in zone_copies + slow_copies:
        copy.wait_send()
    rec_copy.wait_send()
    for level in range(sections):
        forward(level, mine).wait_send()
    for level in range(last):
        swap(level).wait_send()

        @pl.when(level != d)
        def _():
            deliver_copy(level).wait_send()
    for k in range(parts):
        swap_part(k).wait_send()

    @pl.when(d != last)
    def _():
        for k in range(parts):
            deliver_part(k, d).wait_send()
        for other in others:
            pltpu.make_async_remote_copy(
                src_ref=got.at[0], dst_ref=out.at[rows_of(other), :],
                send_sem=grad_send.at[0], recv_sem=grad_recv.at[other],
                device_id=(d, mate_line), device_id_type=MESH,
            ).wait_recv()

    @pl.when(d == last)
    def _():
        for other in others:
            for k in range(parts):
                deliver_part(k, other).wait_recv()


def per_device(
    receiver_data, source_amp, source_x, source_y, omegas, slowness, inverses, zones_x, zones_y
):
    sections = lax.axis_size("depth")
    freqs, _, width_x, width_y = receiver_data.shape
    order = inverses.shape[-1]
    pair = order // width_y
    points = source_x.shape[0]
    zone_count = inverses.shape[1]
    slots = freqs // pair
    assert pair == 2 and sections == 4 and width_x == order * sections and slowness.shape[0] == 1
    vmem = pl.BlockSpec(memory_space=pltpu.VMEM)
    anywhere = pl.BlockSpec(memory_space=pl.ANY)
    dma = pltpu.SemaphoreType.DMA
    out = pl.pallas_call(
        functools.partial(kernel, sections, pair, 32),
        out_shape=pltpu.VMEM((width_x, width_y), BF16),
        in_specs=[anywhere] * 9,
        out_specs=vmem,
        scratch_shapes=[
            pltpu.VMEM((sections, order, order), jnp.int16),
            pltpu.VMEM((width_x, width_y), F32),
            pltpu.VMEM((width_x, width_y), jnp.int16),
            pltpu.VMEM((slots, 2, order, order), BF16),
            pltpu.VMEM((slots, 2, 2, order, order), BF16),
            pltpu.VMEM((slots, zone_count, 2, order, order), BF16),
            pltpu.VMEM((slots, zone_count, 2 * order, 2 * order), BF16),
            pltpu.VMEM(source_amp.shape, BF16),
            pltpu.VMEM((1, points), jnp.int32),
            pltpu.VMEM((1, points), jnp.int32),
            pltpu.SMEM(omegas.shape, F32),
            pltpu.VMEM(zones_x.shape, jnp.int32),
            pltpu.VMEM(zones_y.shape, jnp.int32),
            pltpu.VMEM((8, 128), jnp.int32),
            pltpu.VMEM((sections, 8, 128), jnp.int32),
            pltpu.SMEM((sections, 8, 128), jnp.int32),
            pltpu.VMEM((slots, 2, order, order), BF16),
            pltpu.VMEM((slots, 2 * order, 2 * order), BF16),
            pltpu.VMEM((slots, 2 * order, 2 * order), BF16),
            pltpu.VMEM((sections, order, order), BF16),
            pltpu.VMEM((sections, order, width_y), BF16),
            pltpu.VMEM((order, order), F32),
            dma((sections,)), dma((8,)), dma((sections,)),
            dma((sections,)), dma((sections,)),
            dma((sections,)), dma((sections,)),
            dma((sections,)), dma((sections,)),
            dma, dma,
            dma((sections,)), dma((sections,)),
            dma((PARTS,)), dma((PARTS,)),
            dma((sections,)), dma((sections,)),
            dma((PARTS,)), dma((sections, PARTS)),
            pltpu.SemaphoreType.REGULAR,
        ],
        compiler_params=pltpu.CompilerParams(collective_id=0, has_side_effects=True),
    )(
        receiver_data, source_amp, source_x.reshape(1, points), source_y.reshape(1, points),
        omegas, slowness, inverses, zones_x, zones_y,
    )
    return out.astype(F32)[None]


def solution(mesh):
    in_specs = (
        P(None, None, None, "xline"),
        P(),
        P(),
        P(),
        P(),
        P("depth", None, "xline"),
        P(),
        P("depth", None),
        P("depth", None),
    )
    out_specs = P("depth", None, "xline")
    return jax.shard_map(
        per_device, mesh=mesh, in_specs=in_specs, out_specs=out_specs, check_vma=False
    )
```

```python
import functools
import math

import jax
import jax.numpy as jnp
import numpy as np
from jax import lax
from jax.experimental import pallas as pl
from jax.experimental.pallas import tpu as pltpu
from jax.sharding import PartitionSpec as P

MESH = pl.DeviceIdType.MESH
F32 = jnp.float32
BF16 = jnp.bfloat16

SLOW_LOW, SLOW_HIGH = 0.2, 2.0
OMEGA_LOW, OMEGA_HIGH = 0.5, 3.0
SLOW_MID = 0.5 * (SLOW_LOW + SLOW_HIGH)
CODE_STEP = (SLOW_HIGH - SLOW_LOW) / 65532.0
HALF_SPAN = 0.5 * max(OMEGA_HIGH * SLOW_HIGH - math.pi, math.pi - OMEGA_LOW * SLOW_LOW) + 0.01


def fitted(function, count):
    nodes = np.cos(np.pi * (np.arange(64) + 0.5) / 64)
    square = 0.5 * HALF_SPAN**2 * (nodes + 1.0)
    fit = np.polynomial.Chebyshev.fit(square, function(np.sqrt(square)), count - 1)
    return [float(term) for term in fit.convert(kind=np.polynomial.Polynomial).coef]


PARTS = 2
ROOT2 = math.sqrt(2.0)
SIN_TERMS = fitted(lambda t: ROOT2 * np.sin(t) / t, 4)
COS_TERMS = fitted(lambda t: -ROOT2 * np.cos(t), 5)


def series(square, terms):
    total = square * terms[-1] + terms[-2]
    for term in terms[-3::-1]:
        total = total * square + term
    return total


def sincos(half):
    square = half * half
    root_sine = series(square, SIN_TERMS) * half
    return root_sine * series(square, COS_TERMS), root_sine * root_sine - 1.0


def kernel(
    sections, pair, rows, recv_in, amp_in, src_x_in, src_y_in, omegas_in, slow_in, table_in,
    zones_x_in, zones_y_in,
    out, slow, slow_raw, code, rec, wave, table, forms, amp, src_x, src_y, omegas, zones_x, zones_y,
    zones, zone_buf, zone_rows, trig, rotated, inline, grad, got, total,
    load_sems, local_sems, zone_sems, zone_send, zone_recv, slow_send, slow_recv, fwd_send, fwd_recv,
    rec_send, rec_recv, swap_send, swap_recv, last_send, last_recv, grad_send, grad_recv, tail_send,
    tail_recv, ready,
):
    d = lax.axis_index("depth")
    line = lax.axis_index("xline")
    q = lax.rem(line, pair)
    block = line // pair
    mate_line = line + 1 - 2 * q
    width = recv_in.shape[3]
    order = pair * width
    slots = wave.shape[0]
    last = sections - 1
    parts = last_send.shape[0]

    def rows_of(section):
        return pl.ds(pl.multiple_of(section * order, order), order)

    near = d + 1 - 2 * lax.rem(d, 2)
    next_to = d + 2 - 4 * (d // 2)
    far = last - d
    others = [far, near, next_to]
    FAR, NEAR, NEXT = range(3)

    barrier = pltpu.get_barrier_semaphore()
    for device in ((near, line), (next_to, line), (d, mate_line)):
        pl.semaphore_signal(barrier, inc=1, device_id=device, device_id_type=MESH)

    freqs = pl.ds(q * slots, slots)
    loads = [
        pltpu.make_async_copy(
            slow_in.at[0, rows_of(section), :], slow_raw.at[rows_of(section), :], load_sems.at[k]
        )
        for k, section in enumerate(others + [d])
    ]
    small = [
        pltpu.make_async_copy(source, target, local_sems.at[k])
        for k, (source, target) in enumerate((
            (zones_x_in, zones_x), (zones_y_in, zones_y), (omegas_in, omegas),
            (amp_in, amp), (src_x_in, src_x), (src_y_in, src_y),
        ))
    ]
    rec_load = pltpu.make_async_copy(
        recv_in.at[freqs, :, rows_of(d), :], rec.at[q], local_sems.at[len(small)]
    )
    table_load = pltpu.make_async_copy(
        table_in.at[freqs], table, local_sems.at[len(small) + 1]
    )
    for copy in loads + small + [rec_load]:
        copy.start()

    def encode(section):
        part = rows_of(section)
        scaled = (slow_raw[part, :] - SLOW_MID) * (1.0 / CODE_STEP)
        return jnp.round(scaled).astype(jnp.int32).astype(jnp.int16)

    zones[...] = jnp.zeros_like(zones)
    small[0].wait()
    small[1].wait()
    zones[0:1, 0:zones_x.shape[1]] = zones_x[...]
    zones[1:2, 0:zones_y.shape[1]] = zones_y[...]
    zone_buf[d] = zones[...]
    for k, section in enumerate(others):
        loads[k].wait()
        code[rows_of(section), :] = encode(section)
    loads[len(others)].wait()
    slow[d, q] = encode(d)
    table_load.start()

    zone_copies, slow_copies = [], []
    for k, other in enumerate(others):
        zone_copies.append(
            pltpu.make_async_remote_copy(
                src_ref=zones, dst_ref=zone_buf.at[d], send_sem=zone_send.at[k],
                recv_sem=zone_recv.at[d], device_id=(other, line), device_id_type=MESH,
            )
        )
        slow_copies.append(
            pltpu.make_async_remote_copy(
                src_ref=code.at[rows_of(other), :], dst_ref=slow.at[d, q],
                send_sem=slow_send.at[k], recv_sem=slow_recv.at[d],
                device_id=(other, line), device_id_type=MESH,
            )
        )
    rec_copy = pltpu.make_async_remote_copy(
        src_ref=recv_in.at[pl.ds((1 - q) * slots, slots), :, rows_of(d), :],
        dst_ref=rec.at[q], send_sem=rec_send, recv_sem=rec_recv,
        device_id=(d, mate_line), device_id_type=MESH,
    )

    def share(k):
        zone_copies[k].start()
        slow_copies[k].start()

    def arrived(level):
        zone = pltpu.make_async_remote_copy(
            src_ref=zones, dst_ref=zone_buf.at[level], send_sem=zone_send.at[0],
            recv_sem=zone_recv.at[level], device_id=(d, mate_line), device_id_type=MESH,
        )
        rest = pltpu.make_async_remote_copy(
            src_ref=slow.at[level, q], dst_ref=slow.at[level, q],
            send_sem=slow_send.at[0], recv_sem=slow_recv.at[level],
            device_id=(d, mate_line), device_id_type=MESH,
        )
        return zone, rest

    def forward(level, half):
        return pltpu.make_async_remote_copy(
            src_ref=slow.at[level, half], dst_ref=slow.at[level, half],
            send_sem=fwd_send.at[level], recv_sem=fwd_recv.at[level],
            device_id=(d, mate_line), device_id_type=MESH,
        )

    def zone_copy(level):
        return pltpu.make_async_copy(
            zone_buf.at[level], zone_rows.at[level], zone_sems.at[level]
        )

    def receive(level):
        zone, rest = arrived(level)

        @pl.when(level != d)
        def _():
            zone.wait_recv()
        zone_copy(level).start()

        @pl.when(level != d)
        def _():
            rest.wait_recv()
        forward(level, q).start()

    pl.semaphore_wait(barrier, pair + 1)
    pl.semaphore_signal(ready, inc=1, device_id=(near, line), device_id_type=MESH)

    share(NEAR)
    share(NEXT)
    rec_copy.start()
    for copy in small[2:]:
        copy.wait()

    points = src_x.shape[1]
    cells = lax.broadcasted_iota(jnp.int32, (order, points), 0)
    hit_x = cells + d * order == src_x[...]
    hit_y = jnp.where(cells + block * order == src_y[...], 1.0, 0.0).astype(BF16)
    for slot in range(slots):
        for part in range(2):
            amps = amp[q * slots + slot, pl.ds(part, 1), :].astype(F32)
            spread = jnp.where(hit_x, amps, 0.0).astype(BF16)
            field = lax.dot_general(
                spread, hit_y, (((1,), (1,)), ((), ())), preferred_element_type=F32
            )
            wave[slot, 0, part] = field.astype(BF16)

    pl.semaphore_wait(ready, 1)
    share(FAR)

    table_load.wait()
    for slot in range(slots):
        for zone in range(table.shape[1]):
            k_real, k_imag = table[slot, zone, 0], table[slot, zone, 1]
            forms[slot, zone, :order, :order] = k_real
            forms[slot, zone, :order, order:] = -k_imag
            forms[slot, zone, order:, :order] = k_imag
            forms[slot, zone, order:, order:] = k_real

    def turn(level, half):
        lanes = pl.ds(pl.multiple_of(half * width, width), width)
        for start in range(0, order, rows):
            part = slice(start, start + rows)
            value = slow[level, half, part, :].astype(jnp.int32).astype(F32)
            for slot in range(slots):
                omega = omegas[q * slots + slot]
                slope = omega * (0.5 * CODE_STEP)
                shift = omega * (0.5 * SLOW_MID) - 0.5 * math.pi
                sine, cosine = sincos(value * slope + shift)
                trig[slot, 0, part, lanes] = sine
                trig[slot, 1, part, lanes] = cosine

    def rotate(slot):
        for start in range(0, order, rows):
            part = slice(start, start + rows)
            sine, cosine = trig[slot, 0, part, :], trig[slot, 1, part, :]
            for field in range(2):
                real = wave[slot, field, 0, part, :].astype(F32)
                imag = wave[slot, field, 1, part, :].astype(F32)
                lanes = slice(field * order, (field + 1) * order)
                rotated[slot, part, lanes] = (real * cosine - imag * sine).astype(BF16)
                rotated[slot, order + start:order + start + rows, lanes] = (
                    real * sine + imag * cosine
                ).astype(BF16)

    def solve_inline(level, slot):
        m_x = forms[slot, zone_rows[level, 0, d]]
        for field in range(2):
            lanes = slice(field * order, (field + 1) * order)
            value = rotated[slot, :, lanes]
            added = jnp.dot(m_x, value, preferred_element_type=F32).astype(BF16)
            solved = value + added
            inline[slot, lanes, 0:order] = solved[:order]
            inline[slot, lanes, order:] = solved[order:]

    def solve_crossline(level, slot, part):
        omega = omegas[q * slots + slot]
        m_y = forms[slot, zone_rows[level, 1, block]]
        count = part.stop - part.start
        value = jnp.concatenate(
            [inline[slot, part, :], inline[slot, order + part.start:order + part.stop, :]], axis=0
        )
        product = []
        for half in range(2):
            lanes = slice(half * order, (half + 1) * order)
            added = lax.dot_general(
                value, m_y[lanes], (((1,), (1,)), ((), ())), preferred_element_type=F32
            )
            solved = value[:, lanes] + added.astype(BF16)
            product.append(solved[:count] * solved[count:])
            if level < last:
                wave[slot, 0, half, part] = solved[:count]
                wave[slot, 1, half, part] = solved[count:]
        image = (omega * omega) * (product[0] - product[1]).astype(F32)
        if slot > 0:
            image = total[part, :] + image
        if slot + 1 < slots:
            total[part, :] = image
        else:
            for half in range(pair):
                grad[level, half, part, :] = (
                    image[:, half * width:(half + 1) * width].astype(BF16)
                )

    def swap(level):
        return pltpu.make_async_remote_copy(
            src_ref=grad.at[level, 1 - q], dst_ref=got.at[level],
            send_sem=swap_send.at[level], recv_sem=swap_recv.at[level],
            device_id=(d, mate_line), device_id_type=MESH,
        )

    def swap_part(k):
        part = pl.ds(k * (order // parts), order // parts)
        return pltpu.make_async_remote_copy(
            src_ref=grad.at[last, 1 - q, part], dst_ref=got.at[last, part],
            send_sem=last_send.at[k], recv_sem=last_recv.at[k],
            device_id=(d, mate_line), device_id_type=MESH,
        )

    def deliver_copy(level):
        return pltpu.make_async_remote_copy(
            src_ref=got.at[level], dst_ref=out.at[rows_of(d), :],
            send_sem=grad_send.at[level], recv_sem=grad_recv.at[d],
            device_id=(level, line), device_id_type=MESH,
        )

    def section_part(section, k):
        count = order // parts
        return pl.ds(pl.multiple_of(section * order + k * count, count), count)

    def deliver_part(k, section):
        part = pl.ds(k * (order // parts), order // parts)
        return pltpu.make_async_remote_copy(
            src_ref=got.at[last, part], dst_ref=out.at[section_part(section, k), :],
            send_sem=tail_send.at[k], recv_sem=tail_recv.at[section, k],
            device_id=(last, line), device_id_type=MESH,
        )

    def deliver(level):
        swap(level).wait_recv()
        both = grad[level, q].astype(F32) + got[level].astype(F32)

        @pl.when(level == d)
        def _():
            out[rows_of(d), :] = both.astype(BF16)

        @pl.when(level != d)
        def _():
            got[level] = both.astype(BF16)
            deliver_copy(level).start()

    def deliver_last(k):
        part = pl.ds(k * (order // parts), order // parts)
        swap_part(k).wait_recv()
        both = grad[last, q, part].astype(F32) + got[last, part].astype(F32)

        @pl.when(d == last)
        def _():
            out[section_part(d, k), :] = both.astype(BF16)

        @pl.when(d != last)
        def _():
            got[last, part] = both.astype(BF16)
            deliver_part(k, d).start()

    whole = slice(0, order)
    rec_load.wait()
    rec_copy.wait_recv()
    for slot in range(slots):
        for half in range(pair):
            lanes = slice(half * width, (half + 1) * width)
            wave[slot, 1, 0, :, lanes] = rec[half, slot, 0]
            wave[slot, 1, 1, :, lanes] = -rec[half, slot, 1]
    receive(0)
    turn(0, q)
    receive(1)
    zone_copy(0).wait()
    forward(0, 1 - q).wait_recv()
    turn(0, 1 - q)
    for level in range(sections):
        for slot in range(slots):
            rotate(slot)
            solve_inline(level, slot)
        if level == last:
            break
        if level + 2 < sections:
            receive(level + 2)
        if level > 0:
            deliver(level - 1)
        zone_copy(level + 1).wait()
        forward(level + 1, 1 - q).wait_recv()
        for slot in range(slots):
            solve_crossline(level, slot, whole)
        for half in range(pair):
            turn(level + 1, half)
        swap(level).start()
    for k in range(parts):
        part = slice(k * (order // parts), (k + 1) * (order // parts))
        for slot in range(slots):
            solve_crossline(last, slot, part)
        swap_part(k).start()
        if k == 0:
            deliver(last - 1)
    for k in range(parts):
        deliver_last(k)

    for copy in zone_copies + slow_copies:
        copy.wait_send()
    rec_copy.wait_send()
    for level in range(sections):
        forward(level, q).wait_send()
    for level in range(last):
        swap(level).wait_send()

        @pl.when(level != d)
        def _():
            deliver_copy(level).wait_send()
    for k in range(parts):
        swap_part(k).wait_send()

    @pl.when(d != last)
    def _():
        for k in range(parts):
            deliver_part(k, d).wait_send()
        for other in others:
            pltpu.make_async_remote_copy(
                src_ref=got.at[0], dst_ref=out.at[rows_of(other), :],
                send_sem=grad_send.at[0], recv_sem=grad_recv.at[other],
                device_id=(d, mate_line), device_id_type=MESH,
            ).wait_recv()

    @pl.when(d == last)
    def _():
        for other in others:
            for k in range(parts):
                deliver_part(k, other).wait_recv()


def per_device(
    receiver_data, source_amp, source_x, source_y, omegas, slowness, inverses, zones_x, zones_y
):
    sections = lax.axis_size("depth")
    freqs, _, width_x, width_y = receiver_data.shape
    order = inverses.shape[-1]
    pair = order // width_y
    points = source_x.shape[0]
    zone_count = inverses.shape[1]
    slots = freqs // pair
    assert pair == 2 and sections == 4 and width_x == order * sections and slowness.shape[0] == 1
    vmem = pl.BlockSpec(memory_space=pltpu.VMEM)
    anywhere = pl.BlockSpec(memory_space=pl.ANY)
    dma = pltpu.SemaphoreType.DMA
    out = pl.pallas_call(
        functools.partial(kernel, sections, pair, 32),
        out_shape=pltpu.VMEM((width_x, width_y), BF16),
        in_specs=[anywhere] * 9,
        out_specs=vmem,
        scratch_shapes=[
            pltpu.VMEM((sections, pair, order, width_y), jnp.int16),
            pltpu.VMEM((width_x, width_y), F32),
            pltpu.VMEM((width_x, width_y), jnp.int16),
            pltpu.VMEM((pair, slots, 2, order, width_y), BF16),
            pltpu.VMEM((slots, 2, 2, order, order), BF16),
            pltpu.VMEM((slots, zone_count, 2, order, order), BF16),
            pltpu.VMEM((slots, zone_count, 2 * order, 2 * order), BF16),
            pltpu.VMEM(source_amp.shape, BF16),
            pltpu.VMEM((1, points), jnp.int32),
            pltpu.VMEM((1, points), jnp.int32),
            pltpu.SMEM(omegas.shape, F32),
            pltpu.VMEM(zones_x.shape, jnp.int32),
            pltpu.VMEM(zones_y.shape, jnp.int32),
            pltpu.VMEM((8, 128), jnp.int32),
            pltpu.VMEM((sections, 8, 128), jnp.int32),
            pltpu.SMEM((sections, 8, 128), jnp.int32),
            pltpu.VMEM((slots, 2, order, order), F32),
            pltpu.VMEM((slots, 2 * order, 2 * order), BF16),
            pltpu.VMEM((slots, 2 * order, 2 * order), BF16),
            pltpu.VMEM((sections, pair, order, width_y), BF16),
            pltpu.VMEM((sections, order, width_y), BF16),
            pltpu.VMEM((order, order), F32),
            dma((sections,)), dma((8,)), dma((sections,)),
            dma((sections,)), dma((sections,)),
            dma((sections,)), dma((sections,)),
            dma((sections,)), dma((sections,)),
            dma, dma,
            dma((sections,)), dma((sections,)),
            dma((PARTS,)), dma((PARTS,)),
            dma((sections,)), dma((sections,)),
            dma((PARTS,)), dma((sections, PARTS)),
            pltpu.SemaphoreType.REGULAR,
        ],
        compiler_params=pltpu.CompilerParams(collective_id=0, has_side_effects=True),
    )(
        receiver_data, source_amp, source_x.reshape(1, points), source_y.reshape(1, points),
        omegas, slowness, inverses, zones_x, zones_y,
    )
    return out.astype(F32)[None]


def solution(mesh):
    in_specs = (
        P(None, None, None, "xline"),
        P(),
        P(),
        P(),
        P(),
        P("depth", None, "xline"),
        P(),
        P("depth", None),
        P("depth", None),
    )
    out_specs = P("depth", None, "xline")
    return jax.shard_map(
        per_device, mesh=mesh, in_specs=in_specs, out_specs=out_specs, check_vma=False
    )
```

```python
import functools
import math

import jax
import jax.numpy as jnp
import numpy as np
from jax import lax
from jax.experimental import pallas as pl
from jax.experimental.pallas import tpu as pltpu
from jax.sharding import PartitionSpec as P

MESH = pl.DeviceIdType.MESH
F32 = jnp.float32
BF16 = jnp.bfloat16

SLOW_LOW, SLOW_HIGH = 0.2, 2.0
OMEGA_LOW, OMEGA_HIGH = 0.5, 3.0
SLOW_MID = 0.5 * (SLOW_LOW + SLOW_HIGH)
CODE_STEP = (SLOW_HIGH - SLOW_LOW) / 65532.0
HALF_SPAN = 0.5 * max(OMEGA_HIGH * SLOW_HIGH - math.pi, math.pi - OMEGA_LOW * SLOW_LOW) + 0.01


def fitted(function, count):
    nodes = np.cos(np.pi * (np.arange(64) + 0.5) / 64)
    square = 0.5 * HALF_SPAN**2 * (nodes + 1.0)
    fit = np.polynomial.Chebyshev.fit(square, function(np.sqrt(square)), count - 1)
    return [float(term) for term in fit.convert(kind=np.polynomial.Polynomial).coef]


PARTS = 2
ROOT2 = math.sqrt(2.0)
SIN_TERMS = fitted(lambda t: ROOT2 * np.sin(t) / t, 4)
COS_TERMS = fitted(lambda t: -ROOT2 * np.cos(t), 5)


def series(square, terms):
    total = square * terms[-1] + terms[-2]
    for term in terms[-3::-1]:
        total = total * square + term
    return total


def sincos(half):
    square = half * half
    root_sine = series(square, SIN_TERMS) * half
    return root_sine * series(square, COS_TERMS), root_sine * root_sine - 1.0


def kernel(
    sections, pair, rows, recv_in, amp_in, src_x_in, src_y_in, omegas_in, slow_in, table_in,
    zones_x_in, zones_y_in,
    out, slow, slow_raw, code, rec, wave, table, forms, amp, src_x, src_y, omegas, zones_x, zones_y,
    zones, zone_buf, zone_rows, trig, rotated, inline, grad, got, total,
    load_sems, local_sems, zone_send, zone_recv, slow_send, slow_recv, mate_send, fwd_recv,
    rec_recv, swap_send, grad_send, grad_recv, ready,
):
    d = lax.axis_index("depth")
    line = lax.axis_index("xline")
    q = lax.rem(line, pair)
    block = line // pair
    mate_line = line + 1 - 2 * q
    width = recv_in.shape[3]
    order = pair * width
    slots = wave.shape[0]
    last = sections - 1
    parts = PARTS

    def rows_of(section):
        return pl.ds(pl.multiple_of(section * order, order), order)

    near = d + 1 - 2 * lax.rem(d, 2)
    next_to = d + 2 - 4 * (d // 2)
    far = last - d
    others = [far, near, next_to]
    FAR, NEAR, NEXT = range(3)

    barrier = pltpu.get_barrier_semaphore()
    for device in ((near, line), (next_to, line), (d, mate_line)):
        pl.semaphore_signal(barrier, inc=1, device_id=device, device_id_type=MESH)

    freqs = pl.ds(q * slots, slots)
    loads = [
        pltpu.make_async_copy(
            slow_in.at[0, rows_of(section), :], slow_raw.at[rows_of(section), :], load_sems.at[k]
        )
        for k, section in enumerate(others + [d])
    ]
    small = [
        pltpu.make_async_copy(source, target, local_sems.at[k])
        for k, (source, target) in enumerate((
            (zones_x_in, zones_x), (zones_y_in, zones_y), (omegas_in, omegas),
            (amp_in, amp), (src_x_in, src_x), (src_y_in, src_y),
        ))
    ]
    rec_load = pltpu.make_async_copy(
        recv_in.at[freqs, :, rows_of(d), :], rec.at[q], local_sems.at[len(small)]
    )
    table_load = pltpu.make_async_copy(
        table_in.at[freqs], table, local_sems.at[len(small) + 1]
    )
    for copy in loads + small + [rec_load]:
        copy.start()

    def encode(section):
        part = rows_of(section)
        scaled = (slow_raw[part, :] - SLOW_MID) * (1.0 / CODE_STEP)
        return jnp.round(scaled).astype(jnp.int32).astype(jnp.int16)

    zones[...] = jnp.zeros_like(zones)
    small[0].wait()
    small[1].wait()
    zones[0:1, 0:zones_x.shape[1]] = zones_x[...]
    zones[1:2, 0:zones_y.shape[1]] = zones_y[...]
    zone_buf[d] = zones[...]
    for k, section in enumerate(others):
        loads[k].wait()
        code[rows_of(section), :] = encode(section)
    loads[len(others)].wait()
    slow[d, q] = encode(d)
    table_load.start()

    zone_copies, slow_copies = [], []
    for k, other in enumerate(others):
        zone_copies.append(
            pltpu.make_async_remote_copy(
                src_ref=zones, dst_ref=zone_buf.at[d], send_sem=zone_send,
                recv_sem=zone_recv.at[d], device_id=(other, line), device_id_type=MESH,
            )
        )
        slow_copies.append(
            pltpu.make_async_remote_copy(
                src_ref=code.at[rows_of(other), :], dst_ref=slow.at[d, q],
                send_sem=slow_send, recv_sem=slow_recv.at[d],
                device_id=(other, line), device_id_type=MESH,
            )
        )
    rec_copy = pltpu.make_async_remote_copy(
        src_ref=recv_in.at[pl.ds((1 - q) * slots, slots), :, rows_of(d), :],
        dst_ref=rec.at[q], send_sem=mate_send, recv_sem=rec_recv,
        device_id=(d, mate_line), device_id_type=MESH,
    )

    def share(k):
        zone_copies[k].start()
        slow_copies[k].start()

    def arrived(level):
        zone = pltpu.make_async_remote_copy(
            src_ref=zones, dst_ref=zone_buf.at[level], send_sem=zone_send,
            recv_sem=zone_recv.at[level], device_id=(d, mate_line), device_id_type=MESH,
        )
        rest = pltpu.make_async_remote_copy(
            src_ref=slow.at[level, q], dst_ref=slow.at[level, q],
            send_sem=slow_send, recv_sem=slow_recv.at[level],
            device_id=(d, mate_line), device_id_type=MESH,
        )
        return zone, rest

    def forward(level, half):
        return pltpu.make_async_remote_copy(
            src_ref=slow.at[level, half], dst_ref=slow.at[level, half],
            send_sem=mate_send, recv_sem=fwd_recv.at[level],
            device_id=(d, mate_line), device_id_type=MESH,
        )

    def zone_copy(level):
        return pltpu.make_async_copy(
            zone_buf.at[level], zone_rows.at[level], load_sems.at[level]
        )

    def receive(level):
        zone, rest = arrived(level)

        @pl.when(level != d)
        def _():
            zone.wait_recv()
        zone_copy(level).start()

        @pl.when(level != d)
        def _():
            rest.wait_recv()
        forward(level, q).start()

    pl.semaphore_wait(barrier, pair + 1)
    pl.semaphore_signal(ready, inc=1, device_id=(near, line), device_id_type=MESH)

    share(NEAR)
    share(NEXT)
    rec_copy.start()
    for copy in small[2:]:
        copy.wait()

    points = src_x.shape[1]
    cells = lax.broadcasted_iota(jnp.int32, (order, points), 0)
    hit_x = cells + d * order == src_x[...]
    hit_y = jnp.where(cells + block * order == src_y[...], 1.0, 0.0).astype(BF16)
    for slot in range(slots):
        for part in range(2):
            amps = amp[q * slots + slot, pl.ds(part, 1), :].astype(F32)
            spread = jnp.where(hit_x, amps, 0.0).astype(BF16)
            field = lax.dot_general(
                spread, hit_y, (((1,), (1,)), ((), ())), preferred_element_type=F32
            )
            wave[slot, 0, part] = field.astype(BF16)

    pl.semaphore_wait(ready, 1)
    share(FAR)

    table_load.wait()
    for slot in range(slots):
        for zone in range(table.shape[1]):
            k_real, k_imag = table[slot, zone, 0], table[slot, zone, 1]
            forms[slot, zone, :order, :order] = k_real
            forms[slot, zone, :order, order:] = -k_imag
            forms[slot, zone, order:, :order] = k_imag
            forms[slot, zone, order:, order:] = k_real

    def turn(level, half):
        lanes = pl.ds(pl.multiple_of(half * width, width), width)
        for start in range(0, order, rows):
            part = slice(start, start + rows)
            value = slow[level, half, part, :].astype(jnp.int32).astype(F32)
            for slot in range(slots):
                omega = omegas[q * slots + slot]
                slope = omega * (0.5 * CODE_STEP)
                shift = omega * (0.5 * SLOW_MID) - 0.5 * math.pi
                sine, cosine = sincos(value * slope + shift)
                trig[slot, 0, part, lanes] = sine
                trig[slot, 1, part, lanes] = cosine

    def rotate(slot):
        for start in range(0, order, rows):
            part = slice(start, start + rows)
            sine, cosine = trig[slot, 0, part, :], trig[slot, 1, part, :]
            for field in range(2):
                real = wave[slot, field, 0, part, :].astype(F32)
                imag = wave[slot, field, 1, part, :].astype(F32)
                lanes = slice(field * order, (field + 1) * order)
                rotated[slot, part, lanes] = (real * cosine - imag * sine).astype(BF16)
                rotated[slot, order + start:order + start + rows, lanes] = (
                    real * sine + imag * cosine
                ).astype(BF16)

    def solve_inline(level, slot):
        m_x = forms[slot, zone_rows[level, 0, d]]
        for field in range(2):
            lanes = slice(field * order, (field + 1) * order)
            value = rotated[slot, :, lanes]
            added = jnp.dot(m_x, value, preferred_element_type=F32).astype(BF16)
            solved = value + added
            inline[slot, lanes, 0:order] = solved[:order]
            inline[slot, lanes, order:] = solved[order:]

    def solve_crossline(level, slot, part):
        omega = omegas[q * slots + slot]
        m_y = forms[slot, zone_rows[level, 1, block]]
        count = part.stop - part.start
        value = jnp.concatenate(
            [inline[slot, part, :], inline[slot, order + part.start:order + part.stop, :]], axis=0
        )
        product = []
        for half in range(2):
            lanes = slice(half * order, (half + 1) * order)
            added = lax.dot_general(
                value, m_y[lanes], (((1,), (1,)), ((), ())), preferred_element_type=F32
            )
            solved = value[:, lanes] + added.astype(BF16)
            product.append(solved[:count] * solved[count:])
            if level < last:
                wave[slot, 0, half, part] = solved[:count]
                wave[slot, 1, half, part] = solved[count:]
        image = (omega * omega) * (product[0] - product[1]).astype(F32)
        if slot > 0:
            image = total[part, :] + image
        if slot + 1 < slots:
            total[part, :] = image
        else:
            for half in range(pair):
                grad[level, half, part, :] = (
                    image[:, half * width:(half + 1) * width].astype(BF16)
                )

    def swap(level):
        return pltpu.make_async_remote_copy(
            src_ref=grad.at[level, 1 - q], dst_ref=got.at[level],
            send_sem=swap_send, recv_sem=local_sems.at[level],
            device_id=(d, mate_line), device_id_type=MESH,
        )

    def swap_part(k):
        part = pl.ds(k * (order // parts), order // parts)
        return pltpu.make_async_remote_copy(
            src_ref=grad.at[last, 1 - q, part], dst_ref=got.at[last, part],
            send_sem=swap_send, recv_sem=local_sems.at[last + k],
            device_id=(d, mate_line), device_id_type=MESH,
        )

    def deliver_copy(level):
        return pltpu.make_async_remote_copy(
            src_ref=got.at[level], dst_ref=out.at[rows_of(d), :],
            send_sem=grad_send, recv_sem=grad_recv,
            device_id=(level, line), device_id_type=MESH,
        )

    def section_part(section, k):
        count = order // parts
        return pl.ds(pl.multiple_of(section * order + k * count, count), count)

    def deliver_part(k, section):
        part = pl.ds(k * (order // parts), order // parts)
        return pltpu.make_async_remote_copy(
            src_ref=got.at[last, part], dst_ref=out.at[section_part(section, k), :],
            send_sem=grad_send, recv_sem=grad_recv,
            device_id=(last, line), device_id_type=MESH,
        )

    def deliver(level):
        swap(level).wait_recv()
        both = grad[level, q].astype(F32) + got[level].astype(F32)

        @pl.when(level == d)
        def _():
            out[rows_of(d), :] = both.astype(BF16)

        @pl.when(level != d)
        def _():
            got[level] = both.astype(BF16)
            deliver_copy(level).start()

    def deliver_last(k):
        part = pl.ds(k * (order // parts), order // parts)
        swap_part(k).wait_recv()
        both = grad[last, q, part].astype(F32) + got[last, part].astype(F32)

        @pl.when(d == last)
        def _():
            out[section_part(d, k), :] = both.astype(BF16)

        @pl.when(d != last)
        def _():
            got[last, part] = both.astype(BF16)
            deliver_part(k, d).start()

    whole = slice(0, order)
    rec_load.wait()
    rec_copy.wait_recv()
    for slot in range(slots):
        for half in range(pair):
            lanes = slice(half * width, (half + 1) * width)
            wave[slot, 1, 0, :, lanes] = rec[half, slot, 0]
            wave[slot, 1, 1, :, lanes] = -rec[half, slot, 1]
    receive(0)
    turn(0, q)
    receive(1)
    zone_copy(0).wait()
    forward(0, 1 - q).wait_recv()
    turn(0, 1 - q)
    for level in range(sections):
        for slot in range(slots):
            rotate(slot)
            solve_inline(level, slot)
        if level == last:
            break
        if level + 2 < sections:
            receive(level + 2)
        if level > 0:
            deliver(level - 1)
        zone_copy(level + 1).wait()
        forward(level + 1, 1 - q).wait_recv()
        for slot in range(slots):
            solve_crossline(level, slot, whole)
        for half in range(pair):
            turn(level + 1, half)
        swap(level).start()
    for k in range(parts):
        part = slice(k * (order // parts), (k + 1) * (order // parts))
        for slot in range(slots):
            solve_crossline(last, slot, part)
        swap_part(k).start()
        if k == 0:
            deliver(last - 1)
    for k in range(parts):
        deliver_last(k)

    def all_of(ref, send_sem, recv_sem):
        return pltpu.make_async_remote_copy(
            src_ref=ref, dst_ref=ref, send_sem=send_sem, recv_sem=recv_sem,
            device_id=(d, mate_line), device_id_type=MESH,
        )

    all_of(zone_buf.at[pl.ds(0, last)], zone_send, grad_recv).wait_send()
    all_of(code.at[pl.ds(0, last * order), :], slow_send, grad_recv).wait_send()
    all_of(slow_raw, mate_send, grad_recv).wait_send()
    all_of(grad.at[:, 0], swap_send, grad_recv).wait_send()
    delivered = all_of(got.at[pl.ds(0, last)], grad_send, grad_recv)
    delivered.wait_send()
    delivered.wait_recv()


def per_device(
    receiver_data, source_amp, source_x, source_y, omegas, slowness, inverses, zones_x, zones_y
):
    sections = lax.axis_size("depth")
    freqs, _, width_x, width_y = receiver_data.shape
    order = inverses.shape[-1]
    pair = order // width_y
    points = source_x.shape[0]
    zone_count = inverses.shape[1]
    slots = freqs // pair
    assert slots * 2 == sections and pair == 2 and sections == 4 and width_x == order * sections and slowness.shape[0] == 1
    vmem = pl.BlockSpec(memory_space=pltpu.VMEM)
    anywhere = pl.BlockSpec(memory_space=pl.ANY)
    dma = pltpu.SemaphoreType.DMA
    out = pl.pallas_call(
        functools.partial(kernel, sections, pair, 32),
        out_shape=pltpu.VMEM((width_x, width_y), BF16),
        in_specs=[anywhere] * 9,
        out_specs=vmem,
        scratch_shapes=[
            pltpu.VMEM((sections, pair, order, width_y), jnp.int16),
            pltpu.VMEM((width_x, width_y), F32),
            pltpu.VMEM((width_x, width_y), jnp.int16),
            pltpu.VMEM((pair, slots, 2, order, width_y), BF16),
            pltpu.VMEM((slots, 2, 2, order, order), BF16),
            pltpu.VMEM((slots, zone_count, 2, order, order), BF16),
            pltpu.VMEM((slots, zone_count, 2 * order, 2 * order), BF16),
            pltpu.VMEM(source_amp.shape, BF16),
            pltpu.VMEM((1, points), jnp.int32),
            pltpu.VMEM((1, points), jnp.int32),
            pltpu.SMEM(omegas.shape, F32),
            pltpu.VMEM(zones_x.shape, jnp.int32),
            pltpu.VMEM(zones_y.shape, jnp.int32),
            pltpu.VMEM((8, 128), jnp.int32),
            pltpu.VMEM((sections, 8, 128), jnp.int32),
            pltpu.SMEM((sections, 8, 128), jnp.int32),
            pltpu.VMEM((slots, 2, order, order), F32),
            pltpu.VMEM((slots, 2 * order, 2 * order), BF16),
            pltpu.VMEM((slots, 2 * order, 2 * order), BF16),
            pltpu.VMEM((sections, pair, order, width_y), BF16),
            pltpu.VMEM((sections, order, width_y), BF16),
            pltpu.VMEM((order, order), F32),
            dma((sections,)), dma((8,)),
            dma, dma((sections,)), dma, dma((sections,)),
            dma, dma((sections,)), dma, dma, dma, dma,
            pltpu.SemaphoreType.REGULAR,
        ],
        compiler_params=pltpu.CompilerParams(collective_id=0, has_side_effects=True),
    )(
        receiver_data, source_amp, source_x.reshape(1, points), source_y.reshape(1, points),
        omegas, slowness, inverses, zones_x, zones_y,
    )
    return out.astype(F32)[None]


def solution(mesh):
    in_specs = (
        P(None, None, None, "xline"),
        P(),
        P(),
        P(),
        P(),
        P("depth", None, "xline"),
        P(),
        P("depth", None),
        P("depth", None),
    )
    out_specs = P("depth", None, "xline")
    return jax.shard_map(
        per_device, mesh=mesh, in_specs=in_specs, out_specs=out_specs, check_vma=False
    )
```
